32 devices in a mesh: tm: 8 (over z, x), chan: 4 (over y, core).
Axes of the slice: x: 2, y: 2, z: 4, core: 2. Of those that a mesh axis runs over, the one named last changes fastest.
Arguments:
- surveillance: bfloat16 [128, 1024, 256], P(('chan', 'tm')), parts along dimension 0, may hold values from -6 to 6
- ref_samples: bfloat16 [32, 1040, 256], P('tm'), may hold values from -6 to 6
- block_ids: int32 [32], P('tm'), may hold values from 0 to 31, each once
- walk: int32 [32], P('tm'), may hold values from 0 to 63
- cfar_guard: int32 [2048], P('tm'), may hold values from 1 to 8
- cfar_window: int32 [2048], P('tm'), may hold values from 1 to 16
Outputs:
- detection: float32 [8192, 512], P(('chan', 'tm')), parts along dimension 0
The draws below stay inside these ranges and needn't reach their ends.
There are 4 independent parts, one for each index of `chan`. The reference program is written for one: setup_inputs(seed, part) draws one part's arguments, and reference() takes and returns one part's arrays. A program takes and returns all parts, laid end to end along the dimension named above; an argument that names none is the same for every part. Nothing has to cross between parts.
Inputs may be any that keep to these rules, and one draw needn't show every extreme that they name: block_ids names each of 0 to 31 exactly once.
All inputs are finite; a program needn't handle non-finite values.
Results may differ from the reference program's by a relative error of at most 0.0003.
Values sent between devices are 32-bit elements; how exact they have to be, the bound alone decides.
A program may use at most 64 MiB of HBM per device.

```python
import math
import jax
import jax.numpy as jnp
from jax import lax

D = 2048
DOP = 512
SEGS = 64
GUARD_MAX = 8
WIN_MAX = 16
WALK = 64
NB = 32
L = 131072


def plant(values, own_key, smallest, high):
    place = [jax.random.randint(jax.random.fold_in(own_key, axis), (), 0, length) for axis, length in enumerate(values.shape)]
    main_axis = values.shape.index(max(values.shape))
    neighbour = place[:main_axis] + [(place[main_axis] + 1) % values.shape[main_axis]] + place[main_axis + 1:]
    return values.at[tuple(place)].set(smallest).at[tuple(neighbour)].set(high)


def levels(key, shape, cuts, low, largest):
    gain = 1.0
    for dim, shards_of in cuts:
        heights = jax.random.uniform(jax.random.fold_in(jax.random.fold_in(key, 6), dim), (shards_of,), jnp.float32, low / len(cuts), largest / len(cuts))
        gain = gain * jnp.repeat(jnp.exp(heights), shape[dim] // shards_of).reshape((-1,) + (1,) * (len(shape) - 1 - dim))
    return gain


def gaussian(key, shape, scale, bound, pieces=(), kind=jnp.bfloat16):
    result = jax.random.normal(key, shape, jnp.float32) * scale
    if len(pieces) > 0:
        result = levels(key, shape, pieces, -0.22, 0.18) * result
    return jnp.clip(result, min=-bound, max=bound).astype(kind)


def setup_inputs(seed: int = 0, part: int = 0) -> dict:
    keys = jax.random.split(jax.random.key(seed), 7)
    part_splits = jax.random.split(jax.random.fold_in(keys[6], part), 7)
    surveillance = gaussian(part_splits[0], (NB, L // 128, 256), 1.0, 6.0, ((0, 8),))
    ref_samples = gaussian(keys[1], (NB, (L + D) // 128, 256), 1.0, 6.0, ((0, 8),))
    block_ids = jax.random.permutation(keys[2], NB).astype(jnp.int32)
    walk = plant(jax.random.randint(keys[3], (NB,), 0, WALK), jax.random.fold_in(keys[3], 1), 0, WALK - 1).astype(jnp.int32)
    cfar_guard = plant(jax.random.randint(keys[4], (D,), 1, GUARD_MAX + 1), jax.random.fold_in(keys[4], 1), 1, GUARD_MAX).astype(jnp.int32)
    cfar_window = plant(jax.random.randint(keys[5], (D,), 1, WIN_MAX + 1), jax.random.fold_in(keys[5], 1), 1, WIN_MAX).astype(jnp.int32)
    return dict(surveillance=surveillance, ref_samples=ref_samples, block_ids=block_ids, walk=walk, cfar_guard=cfar_guard, cfar_window=cfar_window)


HIGH = lax.Precision.HIGHEST

def unpack(packed):
    count = packed.shape[0]
    real_part = packed[:, :, :128].astype(jnp.float32).reshape(count, -1)
    imag_part = packed[:, :, 128:].astype(jnp.float32).reshape(count, -1)
    return lax.complex(real_part, imag_part)

def correlate(item):
    surv_line, ref_line, shift = item
    segment = surv_line.reshape(SEGS, D)
    padded = jnp.concatenate([segment, jnp.zeros_like(segment)], axis=1)
    first = ref_line[:SEGS * D].reshape(SEGS, D)
    second = ref_line[D:].reshape(SEGS, D)
    window = jnp.concatenate([first, second], axis=1)
    spectrum = lax.optimization_barrier(jnp.sum(jnp.fft.fft(padded, axis=1) * jnp.conj(jnp.fft.fft(window, axis=1)), axis=0))
    lagged = jnp.fft.ifft(spectrum)
    picked = lax.dynamic_slice_in_dim(lagged, (D - shift).astype(jnp.int32), D)
    keep = jnp.arange(D, dtype=jnp.int32) >= shift
    return (jnp.where(keep, jnp.real(picked), 0.0), jnp.where(keep, jnp.imag(picked), 0.0))

def reference(surveillance, ref_samples, block_ids, walk, cfar_guard, cfar_window):
    real_c, imag_c = lax.map(correlate, (unpack(surveillance), unpack(ref_samples), walk))
    norm = 1.0 / math.sqrt(NB * SEGS * D)
    freq = jnp.arange(DOP, dtype=jnp.int32)
    theta = 2.0 * math.pi / DOP * (block_ids[:, None] * freq[None, :] % DOP).astype(jnp.float32)
    cos_table = jnp.cos(theta)
    sin_table = jnp.sin(theta)
    amp_re = (jnp.dot(real_c.T, cos_table, precision=HIGH) + jnp.dot(imag_c.T, sin_table, precision=HIGH)) * norm
    amp_im = (jnp.dot(imag_c.T, cos_table, precision=HIGH) - jnp.dot(real_c.T, sin_table, precision=HIGH)) * norm
    power = amp_re * amp_re + amp_im * amp_im
    floor = lax.optimization_barrier(jnp.sum(real_c * real_c + imag_c * imag_c, axis=0)) / (NB * SEGS * D)
    guard = cfar_guard
    width = cfar_window
    reach = GUARD_MAX + WIN_MAX
    padded = jnp.pad(power, ((reach, reach), (0, 0)))
    valid = jnp.pad(jnp.ones((D,), jnp.float32), (reach, reach))
    delay_sum = jnp.zeros_like(power)
    doppler_sum = jnp.zeros_like(power)
    count = jnp.zeros((D,), jnp.float32)
    for step in range(1, reach + 1):
        active = ((step > guard) & (step <= guard + width)).astype(jnp.float32)
        delay_sum = delay_sum + active[:, None] * (padded[reach + step:reach + step + D] + padded[reach - step:reach - step + D])
        count = count + active * (valid[reach + step:reach + step + D] + valid[reach - step:reach - step + D])
        doppler_sum = doppler_sum + active[:, None] * (jnp.roll(power, -step, axis=1) + jnp.roll(power, step, axis=1))
    noise = (delay_sum + doppler_sum) / (count[:, None] + 2.0 * width.astype(jnp.float32)[:, None])
    return (power - floor[:, None]) / (0.25 + noise)
```

```python
import functools
import math

import numpy as np
import jax
import jax.numpy as jnp
from jax import lax
from jax.experimental import pallas as pl
from jax.experimental.pallas import tpu as pltpu
from jax.sharding import PartitionSpec as P

D = 2048
DOP = 512
SEGS = 64
GUARD_MAX = 8
WIN_MAX = 16
REACH = GUARD_MAX + WIN_MAX
LANES = 128
SEG_ROWS = D // LANES
CHUNK = SEG_ROWS * SEG_ROWS
MESH = pl.DeviceIdType.MESH
F32 = jnp.float32
BF16 = jnp.bfloat16


def window_rows(span):
    starts = range(0, D, span)
    return max((s + span + REACH - 1) // LANES - (s - REACH) // LANES + 1 for s in starts)


def iota(shape, dim):
    return lax.broadcasted_iota(jnp.int32, shape, dim)


def split(x):
    high = x.astype(BF16)
    return high, (x - high.astype(F32)).astype(BF16)


def mm(a, b, dims=((1,), (0,))):
    return lax.dot_general(a, b, (dims, ((), ())), preferred_element_type=F32)


def mm3(a, high, low):
    a_high, a_low = split(a)
    return mm(a_high, high) + (mm(a_low, high) + mm(a_high, low))


def correlate_kernel(span, walk_ref, ids_ref, s_ref, e_ref, out_ref, lhs_ref, rhs_ref, diag_ref, prev_ref):
    block = pl.program_id(0)
    chunks = s_ref.shape[1] // CHUNK
    devices, rows_sent = out_ref.shape[0], out_ref.shape[1] - 1
    blocks = out_ref.shape[2] // 2

    @pl.when(block == 0)
    def _():
        out_ref[...] = jnp.zeros_like(out_ref)
        ids = jnp.concatenate(
            [jnp.full((2, LANES), ids_ref[j], jnp.int32) for j in range(blocks)], 0
        ).astype(F32)
        for dev in range(devices):
            out_ref[dev, rows_sent] = ids

    q, row = iota((CHUNK, CHUNK), 0), iota((CHUNK, CHUNK), 1)
    swap = jnp.where(row == (q % SEG_ROWS) * SEG_ROWS + q // SEG_ROWS, 1.0, 0.0).astype(BF16)
    for ch in range(chunks):
        at = ch * CHUNK
        turned = mm(s_ref[0, at : at + CHUNK, :], swap, ((0,), (0,)))
        lhs_ref[:, at : at + CHUNK] = turned.astype(BF16)
        rhs_ref[ch, :CHUNK, :] = mm(swap, e_ref[0, at : at + CHUNK, :]).astype(BF16)
        late = at + SEG_ROWS
        rhs_ref[ch, CHUNK:, :] = mm(swap, e_ref[0, late : late + CHUNK, :]).astype(BF16)

    def product(a):
        off = pl.multiple_of((SEG_ROWS - a) * SEG_ROWS, SEG_ROWS)
        rhs = jnp.concatenate([rhs_ref[ch, pl.ds(off, CHUNK), :] for ch in range(chunks)], 0)
        g = mm(lhs_ref[...], rhs)
        return (
            g[:LANES, :LANES] + g[LANES:, LANES:],
            g[LANES:, :LANES] - g[:LANES, LANES:],
        )

    lower = iota((LANES, LANES), 1) <= iota((LANES, LANES), 0)
    prev_ref[0], prev_ref[1] = product(SEG_ROWS)
    group = 4

    def step(i, carry):
        later = [prev_ref[0], prev_ref[1]]
        for u in range(group):
            a = SEG_ROWS - 1 - (i * group + u)
            here = product(a)
            for part in range(2):
                x = jnp.where(lower, here[part], later[part])
                half = LANES // 2
                while half >= 8:
                    x = x[:half] + pltpu.roll(x[half:], LANES - half, 1)
                    half //= 2
                diag_ref[part, a] = x
            later = here
        prev_ref[0], prev_ref[1] = later
        return carry

    lax.fori_loop(0, SEG_ROWS // group, step, 0)

    x = diag_ref[...].reshape(2 * SEG_ROWS * 8, LANES)
    sub = iota(x.shape, 0) % 8
    for bit in (4, 2, 1):
        x = jnp.where((sub & bit) != 0, pltpu.roll(x, LANES - bit, 1), x)
    x = jnp.sum(x.reshape(2 * SEG_ROWS, 8, LANES), axis=1)
    shift = walk_ref[block]
    place = iota((LANES, LANES), 0) + iota((LANES, LANES), 1) - shift
    turn = jnp.where(place % LANES == 0, 1.0, 0.0).astype(BF16)
    high, rest = x.astype(BF16), None
    rest = x - high.astype(F32)
    mid, low = split(rest)
    x = mm(high, turn) + (mm(mid, turn) + mm(low, turn))
    before = iota((SEG_ROWS, LANES), 1) < shift
    for part in range(2):
        own = x[part * SEG_ROWS : (part + 1) * SEG_ROWS]
        above = jnp.concatenate([jnp.zeros((1, LANES), F32), own[: SEG_ROWS - 1]], 0)
        own = jnp.where(before, above, own)
        slot = 2 * block + part
        for dev in range(devices):
            first = (dev * span - REACH) // LANES
            for r in range(rows_sent):
                if 0 <= first + r < SEG_ROWS:
                    out_ref[dev, r, pl.ds(slot, 1), :] = own[first + r : first + r + 1]


def cosine(count):
    wrapped = (count + DOP // 2) % DOP - DOP // 2
    z = (DOP // 4 - jnp.abs(wrapped)).astype(F32) * (2.0 * math.pi / DOP)
    z2 = z * z
    poly = -1.0 / 39916800.0
    for c in (1.0 / 362880.0, -1.0 / 5040.0, 1.0 / 120.0, -1.0 / 6.0, 1.0):
        poly = poly * z2 + c
    return z * poly


def map_kernel(
    devices, span, send_ref, cfar_ref, dft_high, dft_low, tab_high, tab_low, ker_high, ker_low,
    out_ref, got, power_ref, coef_ref, send_sem, recv_sem,
):
    me = lax.axis_index("tm")
    rows_sent = send_ref.shape[1] - 1
    per = send_ref.shape[2]
    total = devices * per // 2
    barrier = pltpu.get_barrier_semaphore()
    peers = [lax.rem(me + k, devices) for k in range(1, devices)]
    for peer in peers:
        pl.semaphore_signal(barrier, inc=1, device_id={"tm": peer}, device_id_type=MESH)
    pl.semaphore_wait(barrier, devices - 1)
    copies = []
    for k, peer in enumerate(peers):
        copy = pltpu.make_async_remote_copy(
            src_ref=send_ref.at[peer],
            dst_ref=got.at[me],
            send_sem=send_sem.at[k],
            recv_sem=recv_sem.at[k],
            device_id={"tm": peer},
            device_id_type=MESH,
        )
        copy.start()
        copies.append(copy)
    got[me] = send_ref[me]

    width_all = rows_sent * LANES
    if span % LANES == 0:
        crop, lead = LANES - 32, 32
        width = span + 64
    else:
        crop, width = 0, width_all
        base = me * span - REACH + 2 * LANES
        lead = pl.multiple_of(base % LANES + REACH, 8)
    guard = cfar_ref[0:1, :].astype(F32)
    size = cfar_ref[1:2, :].astype(F32)
    guard = jnp.transpose(jnp.broadcast_to(guard, (LANES, span)))
    outer = guard + jnp.transpose(jnp.broadcast_to(size, (LANES, span)))
    dist = iota((span, LANES), 1).astype(F32)
    inside = jnp.where((dist > guard) & (dist <= outer), 1.0, 0.0).astype(BF16)
    kernel = mm(inside, ker_high[...]) + mm(inside, ker_low[...])
    guard, outer = guard[:, :1], outer[:, :1]
    dist = jnp.abs(iota((span, width), 1) - lead - iota((span, width), 0)).astype(F32)
    band = jnp.where((dist > guard) & (dist <= outer), 1.0, 0.0).astype(BF16)
    spot = (me * span + iota((span, 1), 0)).astype(F32)
    last = (D - 1) - spot
    count = jnp.minimum(spot, outer) - jnp.minimum(spot, guard)
    count = count + jnp.minimum(last, outer) - jnp.minimum(last, guard)
    weight = 1.0 / (count + 2.0 * (outer - guard))

    for copy in copies:
        copy.wait()
    stacked = jnp.concatenate(
        [
            jnp.concatenate([got[dev, r] for r in range(rows_sent)], 1)
            for dev in range(devices)
        ],
        0,
    )
    ids = jnp.concatenate([got[dev, rows_sent] for dev in range(devices)], 0)
    ids = ids[:, :1].astype(jnp.int32)
    shape = (devices * per, DOP)
    turns = ids * iota(shape, 1) - (DOP // 4) * (iota(shape, 0) % 2)
    mix_re_high, mix_re_low = split(cosine(turns))
    mix_im_high, mix_im_low = split(cosine(turns + DOP // 4))
    corr = jnp.transpose(stacked)[crop : crop + width]
    corr_high, corr_low = split(corr)
    norm = 1.0 / (total * SEGS * D)
    re = mm(corr_high, mix_re_high) + (mm(corr_low, mix_re_high) + mm(corr_high, mix_re_low))
    im = mm(corr_high, mix_im_high) + (mm(corr_low, mix_im_high) + mm(corr_high, mix_im_low))
    power = (re * re + im * im) * norm
    floor = jnp.sum(corr * corr, axis=1, keepdims=True) * norm
    coef = mm3(power, dft_high[...], dft_low[...])
    if span % LANES == 0:
        power_c = power[lead : lead + span]
        coef_c = coef[lead : lead + span]
        floor_c = floor[lead : lead + span]
    else:
        power_ref[:, :DOP] = power
        power_ref[:, DOP:] = jnp.broadcast_to(floor, (width, LANES))
        coef_ref[...] = coef
        power_c = power_ref[pl.ds(lead, span), :DOP]
        floor_c = power_ref[pl.ds(lead, span), DOP:][:, :1]
        coef_c = coef_ref[pl.ds(lead, span), :]
    coef_high, coef_low = split(coef)
    sums = mm(band, coef_high) + mm(band, coef_low) + coef_c * kernel
    noise = mm3(sums, tab_high[...], tab_low[...]) * weight
    out_ref[...] = (power_c - floor_c) / (0.25 + noise)


def np_split(x):
    high = x.astype(BF16)
    return jnp.asarray(high), jnp.asarray((x - high.astype(np.float64)).astype(BF16))


def tables(total):
    lag, freq = np.arange(total), np.arange(DOP)
    angle = 2.0 * np.pi / DOP * ((lag[:, None] * freq[None, :]) % DOP)
    tab = np.concatenate([np.cos(angle), np.sin(angle)], 0)
    scale = np.where(lag == 0, 1.0, 2.0) / DOP
    dft = tab.T * np.concatenate([scale, scale])[None, :]
    dist = np.arange(LANES)
    ker = 2.0 * np.cos(2.0 * np.pi / DOP * ((dist[:, None] * lag[None, :]) % DOP))
    ker = np.concatenate([ker, ker], 1)
    return (*np_split(dft), *np_split(tab), *np_split(ker))


def body(surveillance, ref_samples, block_ids, walk, cfar_guard, cfar_window):
    blocks, rows_all = surveillance.shape[:2]
    devices = lax.axis_size("tm")
    total = blocks * devices
    span = D // devices
    rows_sent = window_rows(span)
    chunks = rows_all // CHUNK
    send_shape = (devices, rows_sent + 1, 2 * blocks, LANES)
    smem = pl.BlockSpec(memory_space=pltpu.SMEM)
    vmem = pl.BlockSpec(memory_space=pltpu.VMEM)
    windows = pl.pallas_call(
        functools.partial(correlate_kernel, span),
        grid=(blocks,),
        out_shape=jax.ShapeDtypeStruct(send_shape, F32),
        in_specs=[
            smem,
            smem,
            pl.BlockSpec((1,) + surveillance.shape[1:], lambda j: (j, 0, 0)),
            pl.BlockSpec((1,) + ref_samples.shape[1:], lambda j: (j, 0, 0)),
        ],
        out_specs=pl.BlockSpec(send_shape, lambda j: (0, 0, 0, 0)),
        scratch_shapes=[
            pltpu.VMEM((2 * LANES, rows_all), BF16),
            pltpu.VMEM((chunks, 2 * CHUNK, 2 * LANES), BF16),
            pltpu.VMEM((2, SEG_ROWS, 8, LANES), F32),
            pltpu.VMEM((2, LANES, LANES), F32),
        ],
        compiler_params=pltpu.CompilerParams(dimension_semantics=("arbitrary",)),
        name="correlate",
    )(walk, block_ids, surveillance, ref_samples)
    width = span + 64 if span % LANES == 0 else rows_sent * LANES
    cfar = jnp.stack([cfar_guard, cfar_window])
    consts = tables(total)
    return pl.pallas_call(
        functools.partial(map_kernel, devices, span),
        out_shape=jax.ShapeDtypeStruct((span, DOP), F32),
        in_specs=[vmem] * 8,
        out_specs=vmem,
        scratch_shapes=[
            pltpu.VMEM(send_shape, F32),
            pltpu.VMEM((width, DOP + LANES), F32),
            pltpu.VMEM((width, 2 * total), F32),
            pltpu.SemaphoreType.DMA((devices,)),
            pltpu.SemaphoreType.DMA((devices,)),
        ],
        compiler_params=pltpu.CompilerParams(collective_id=0, has_side_effects=True),
        name="map",
    )(windows, cfar, *consts)


def solution(mesh):
    in_specs = (
        P(("chan", "tm"), None, None),
        P("tm", None, None),
        P("tm"),
        P("tm"),
        P("tm"),
        P("tm"),
    )
    out_specs = P(("chan", "tm"), None)
    return jax.shard_map(body, mesh=mesh, in_specs=in_specs, out_specs=out_specs, check_vma=False)
```

```python
import functools
import math

import numpy as np
import jax
import jax.numpy as jnp
from jax import lax
from jax.experimental import pallas as pl
from jax.experimental.pallas import tpu as pltpu
from jax.sharding import PartitionSpec as P

D = 2048
DOP = 512
SEGS = 64
GUARD_MAX = 8
WIN_MAX = 16
REACH = GUARD_MAX + WIN_MAX
LANES = 128
SEG_ROWS = D // LANES
CHUNK = SEG_ROWS * SEG_ROWS
MESH = pl.DeviceIdType.MESH
F32 = jnp.float32
BF16 = jnp.bfloat16


def window_rows(span):
    return max(s % LANES + span + 2 * REACH for s in range(0, D, span)) // LANES + 1


def iota(shape, dim):
    return lax.broadcasted_iota(jnp.int32, shape, dim)


def split(x):
    high = x.astype(BF16)
    return high, (x - high.astype(F32)).astype(BF16)


def mm(a, b, dims=((1,), (0,))):
    return lax.dot_general(a, b, (dims, ((), ())), preferred_element_type=F32)


def mm3(a, high, low):
    a_high, a_low = split(a)
    return mm(a_high, high) + (mm(a_low, high) + mm(a_high, low))


def correlate_kernel(
    span, walk_ref, ids_ref, s_ref, e_ref, swap_ref, pick_ref, out_ref,
    lhs_ref, rhs_ref, diag_ref, send, got, send_sem, recv_sem,
):
    block = pl.program_id(0)
    chunks = s_ref.shape[1] // CHUNK
    devices, rows_sent = out_ref.shape[0], out_ref.shape[1]
    blocks = out_ref.shape[2] // 2
    me = lax.axis_index("tm")
    barrier = pltpu.get_barrier_semaphore()
    peers = [lax.rem(me + k, devices) for k in range(1, devices)]

    @pl.when(block == 0)
    def _():
        for peer in peers:
            pl.semaphore_signal(barrier, inc=1, device_id={"tm": peer}, device_id_type=MESH)
        send[...] = jnp.zeros_like(send)

    swap = swap_ref[...]
    for ch in range(chunks):
        at = ch * CHUNK
        turned = mm(s_ref[0, at : at + CHUNK, :], swap, ((0,), (0,)))
        lhs_ref[:, at : at + CHUNK] = turned.astype(BF16)
        late = at + SEG_ROWS
        rhs_ref[ch, CHUNK:, :] = mm(swap, e_ref[0, late : late + CHUNK, :]).astype(BF16)
        rhs_ref[ch, :CHUNK, :] = mm(swap, e_ref[0, at : at + CHUNK, :]).astype(BF16)

    def product(a):
        off = (SEG_ROWS - a) * SEG_ROWS
        rhs = jnp.concatenate([rhs_ref[ch, off : off + CHUNK, :] for ch in range(chunks)], 0)
        g = mm(lhs_ref[...], rhs)
        return (
            g[:LANES, :LANES] + g[LANES:, LANES:],
            g[LANES:, :LANES] - g[:LANES, LANES:],
        )

    lower = iota((LANES, LANES), 1) <= iota((LANES, LANES), 0)
    later = product(SEG_ROWS)
    for a in reversed(range(SEG_ROWS)):
        here = product(a)
        for part in range(2):
            x = jnp.where(lower, here[part], later[part])
            half = LANES // 2
            while half >= 8:
                x = x[:half] + pltpu.roll(x[half:], LANES - half, 1)
                half //= 2
            diag_ref[part, a] = x
        later = here

    x = diag_ref[...].reshape(2 * SEG_ROWS * 8, LANES)
    sub = iota(x.shape, 0)
    for bit in (4, 2, 1):
        x = jnp.where((sub & bit) != 0, pltpu.roll(x, LANES - bit, 1), x)
    high, low = split(x)
    x = mm(pick_ref[...], high) + mm(pick_ref[...], low)
    shift = walk_ref[block] + REACH
    place = iota((LANES, LANES), 0) + iota((LANES, LANES), 1) - shift
    turn = jnp.where((place & (LANES - 1)) == 0, 1.0, 0.0).astype(BF16)
    high = x.astype(BF16)
    mid, low = split(x - high.astype(F32))
    x = mm(high, turn) + (mm(mid, turn) + mm(low, turn))
    lane = iota((SEG_ROWS, LANES), 1)
    label = jnp.full((1, LANES), ids_ref[block], jnp.int32).astype(F32)
    zero = jnp.zeros((1, LANES), F32)
    for part in range(2):
        own = x[part * SEG_ROWS : (part + 1) * SEG_ROWS]
        above = jnp.concatenate([zero, own[: SEG_ROWS - 1]], 0)
        tail = jnp.where(lane[:1] < REACH, own[SEG_ROWS - 1 :], 0.0)
        own = jnp.where(lane < shift, above, own)
        slot = 2 * block + part
        for dev in range(devices):
            first = dev * span // LANES
            for r in range(rows_sent):
                at = first + r
                row = own[at : at + 1] if at < SEG_ROWS else tail if at == SEG_ROWS else zero
                if r == rows_sent - 1:
                    row = jnp.where(lane[:1] == LANES - 1, label, row)
                send[dev, r, pl.ds(slot, 1), :] = row

    @pl.when(block == blocks - 1)
    def _():
        pl.semaphore_wait(barrier, devices - 1)
        copies = []
        for k, peer in enumerate(peers):
            copy = pltpu.make_async_remote_copy(
                src_ref=send.at[peer],
                dst_ref=got.at[me],
                send_sem=send_sem.at[k],
                recv_sem=recv_sem.at[k],
                device_id={"tm": peer},
                device_id_type=MESH,
            )
            copy.start()
            copies.append(copy)
        got[me] = send[me]
        for copy in copies:
            copy.wait()
        out_ref[...] = got[...]


def cosine(count):
    wrapped = ((count + DOP // 2) & (DOP - 1)) - DOP // 2
    z = (DOP // 4 - jnp.abs(wrapped)).astype(F32) * (2.0 * math.pi / DOP)
    z2 = z * z
    poly = -1.0 / 39916800.0
    for c in (1.0 / 362880.0, -1.0 / 5040.0, 1.0 / 120.0, -1.0 / 6.0, 1.0):
        poly = poly * z2 + c
    return z * poly


def map_kernel(
    span, got, guard_ref, size_ref, dft_high, dft_low, tab_high, tab_low, ker_high, ker_low,
    out_ref, power_ref, coef_ref,
):
    me = lax.axis_index("tm")
    devices, rows_sent, per = got.shape[:3]
    total = devices * per // 2
    if span % LANES == 0:
        lead, width = REACH, span + 2 * REACH
    else:
        width = rows_sent * LANES
        lead = pl.multiple_of(lax.rem(me * span, LANES) + REACH, 8)
    guard = guard_ref[...].astype(F32)
    size = size_ref[...].astype(F32)
    guard = jnp.transpose(jnp.broadcast_to(guard, (LANES, span)))
    outer = guard + jnp.transpose(jnp.broadcast_to(size, (LANES, span)))
    dist = iota((span, LANES), 1).astype(F32)
    inside = jnp.where((dist > guard) & (dist <= outer), 1.0, 0.0).astype(BF16)
    kernel = mm(inside, ker_high[...]) + mm(inside, ker_low[...])
    guard, outer = guard[:, :1], outer[:, :1]
    dist = jnp.abs(iota((span, width), 1) - lead - iota((span, width), 0)).astype(F32)
    band = jnp.where((dist > guard) & (dist <= outer), 1.0, 0.0).astype(BF16)
    spot = (me * span + iota((span, 1), 0)).astype(F32)
    last = (D - 1) - spot
    count = jnp.minimum(spot, outer) - jnp.minimum(spot, guard)
    count = count + jnp.minimum(last, outer) - jnp.minimum(last, guard)
    weight = 1.0 / (count + 2.0 * (outer - guard))

    rows = [[got[dev, r] for r in range(rows_sent)] for dev in range(devices)]
    stacked = jnp.concatenate([jnp.concatenate(r, 1) for r in rows], 0)
    ids = stacked[:, rows_sent * LANES - 1 :].astype(jnp.int32)
    shape = (devices * per, DOP)
    turns = ids * iota(shape, 1) - (DOP // 4) * (iota(shape, 0) & 1)
    mix_re_high, mix_re_low = split(cosine(turns))
    mix_im_high, mix_im_low = split(cosine(turns + DOP // 4))
    corr = jnp.transpose(stacked)[:width]
    corr_high, corr_low = split(corr)
    norm = 1.0 / (total * SEGS * D)
    re = mm(corr_high, mix_re_high) + (mm(corr_low, mix_re_high) + mm(corr_high, mix_re_low))
    im = mm(corr_high, mix_im_high) + (mm(corr_low, mix_im_high) + mm(corr_high, mix_im_low))
    power = (re * re + im * im) * norm
    floor = jnp.sum(corr * corr, axis=1, keepdims=True) * norm
    coef = mm3(power, dft_high[...], dft_low[...])
    if span % LANES == 0:
        power_c = power[lead : lead + span]
        coef_c = coef[lead : lead + span]
        floor_c = floor[lead : lead + span]
    else:
        power_ref[:, :DOP] = power
        power_ref[:, DOP:] = jnp.broadcast_to(floor, (width, LANES))
        coef_ref[...] = coef
        power_c = power_ref[pl.ds(lead, span), :DOP]
        floor_c = power_ref[pl.ds(lead, span), DOP:][:, :1]
        coef_c = coef_ref[pl.ds(lead, span), :]
    coef_high, coef_low = split(coef)
    sums = mm(band, coef_high) + mm(band, coef_low) + coef_c * kernel
    noise = mm3(sums, tab_high[...], tab_low[...]) * weight
    out_ref[...] = (power_c - floor_c) / (0.25 + noise)


def np_split(x):
    high = x.astype(BF16)
    return jnp.asarray(high), jnp.asarray((x - high.astype(np.float64)).astype(BF16))


def tables(total):
    lag, freq = np.arange(total), np.arange(DOP)
    angle = 2.0 * np.pi / DOP * ((lag[:, None] * freq[None, :]) % DOP)
    tab = np.concatenate([np.cos(angle), np.sin(angle)], 0)
    scale = np.where(lag == 0, 1.0, 2.0) / DOP
    dft = tab.T * np.concatenate([scale, scale])[None, :]
    dist = np.arange(LANES)
    ker = 2.0 * np.cos(2.0 * np.pi / DOP * ((dist[:, None] * lag[None, :]) % DOP))
    ker = np.concatenate([ker, ker], 1)
    return (*np_split(dft), *np_split(tab), *np_split(ker))


def body(surveillance, ref_samples, block_ids, walk, cfar_guard, cfar_window):
    blocks, rows_all = surveillance.shape[:2]
    devices = lax.axis_size("tm")
    total = blocks * devices
    span = D // devices
    rows_sent = window_rows(span)
    chunks = rows_all // CHUNK
    send_shape = (devices, rows_sent, 2 * blocks, LANES)
    smem = pl.BlockSpec(memory_space=pltpu.SMEM)
    vmem = pl.BlockSpec(memory_space=pltpu.VMEM)
    place = np.arange(CHUNK)
    swap = place[None, :] == (place % SEG_ROWS * SEG_ROWS + place // SEG_ROWS)[:, None]
    pick = np.arange(2 * SEG_ROWS)[:, None] == (np.arange(16 * SEG_ROWS) // 8)[None, :]
    windows = pl.pallas_call(
        functools.partial(correlate_kernel, span),
        grid=(blocks,),
        out_shape=jax.ShapeDtypeStruct(send_shape, F32),
        in_specs=[
            smem,
            smem,
            pl.BlockSpec((1,) + surveillance.shape[1:], lambda j: (j, 0, 0)),
            pl.BlockSpec((1,) + ref_samples.shape[1:], lambda j: (j, 0, 0)),
            vmem,
            vmem,
        ],
        out_specs=vmem,
        scratch_shapes=[
            pltpu.VMEM((2 * LANES, rows_all), BF16),
            pltpu.VMEM((chunks, 2 * CHUNK, 2 * LANES), BF16),
            pltpu.VMEM((2, SEG_ROWS, 8, LANES), F32),
            pltpu.VMEM(send_shape, F32),
            pltpu.VMEM(send_shape, F32),
            pltpu.SemaphoreType.DMA((devices,)),
            pltpu.SemaphoreType.DMA((devices,)),
        ],
        compiler_params=pltpu.CompilerParams(
            dimension_semantics=("arbitrary",), collective_id=0, has_side_effects=True
        ),
        name="correlate",
    )(walk, block_ids, surveillance, ref_samples, jnp.asarray(swap.astype(BF16)), jnp.asarray(pick.astype(BF16)))
    width = span + 2 * REACH if span % LANES == 0 else rows_sent * LANES
    return pl.pallas_call(
        functools.partial(map_kernel, span),
        out_shape=jax.ShapeDtypeStruct((span, DOP), F32),
        in_specs=[vmem] * 9,
        out_specs=vmem,
        scratch_shapes=[
            pltpu.VMEM((width, DOP + LANES), F32),
            pltpu.VMEM((width, 2 * total), F32),
        ],
        name="map",
    )(windows, cfar_guard.reshape(1, span), cfar_window.reshape(1, span), *tables(total))


def solution(mesh):
    in_specs = (
        P(("chan", "tm"), None, None),
        P("tm", None, None),
        P("tm"),
        P("tm"),
        P("tm"),
        P("tm"),
    )
    out_specs = P(("chan", "tm"), None)
    return jax.shard_map(body, mesh=mesh, in_specs=in_specs, out_specs=out_specs, check_vma=False)
```

```python
import functools
import math

import numpy as np
import jax
import jax.numpy as jnp
from jax import lax
from jax.experimental import pallas as pl
from jax.experimental.pallas import tpu as pltpu
from jax.sharding import PartitionSpec as P

D = 2048
DOP = 512
SEGS = 64
GUARD_MAX = 8
WIN_MAX = 16
REACH = GUARD_MAX + WIN_MAX
LANES = 128
SEG_ROWS = D // LANES
CHUNK = SEG_ROWS * SEG_ROWS
MESH = pl.DeviceIdType.MESH
F32 = jnp.float32
BF16 = jnp.bfloat16


def window_rows(span):
    return max(s % LANES + span + 2 * REACH for s in range(0, D, span)) // LANES + 1


def iota(shape, dim):
    return lax.broadcasted_iota(jnp.int32, shape, dim)


def split(x):
    high = x.astype(BF16)
    return high, (x - high.astype(F32)).astype(BF16)


def mm(a, b, dims=((1,), (0,))):
    return lax.dot_general(a, b, (dims, ((), ())), preferred_element_type=F32)


def mm3(a, high, low):
    a_high, a_low = split(a)
    return mm(a_high, high) + (mm(a_low, high) + mm(a_high, low))


def correlate_kernel(
    span, walk_ref, ids_ref, s_ref, e_ref, swap_ref, pick_ref, out_ref,
    lhs_ref, rhs_ref, diag_ref, send, got, send_sem, recv_sem,
):
    block = pl.program_id(0)
    chunks = s_ref.shape[1] // CHUNK
    devices, rows_sent = out_ref.shape[0], out_ref.shape[1]
    blocks = out_ref.shape[2] // 2
    me = lax.axis_index("tm")
    barrier = pltpu.get_barrier_semaphore()
    peers = [lax.rem(me + k, devices) for k in range(1, devices)]

    @pl.when(block == 0)
    def _():
        for peer in peers:
            pl.semaphore_signal(barrier, inc=1, device_id={"tm": peer}, device_id_type=MESH)
        diag_ref[...] = jnp.zeros_like(diag_ref)

    def finish(done):
        x = diag_ref[...].reshape(2 * SEG_ROWS * 8, LANES)
        sub = iota(x.shape, 0)
        for bit in (4, 2, 1):
            x = jnp.where((sub & bit) != 0, pltpu.roll(x, LANES - bit, 1), x)
        high, low = split(x)
        x = mm(pick_ref[...], high) + mm(pick_ref[...], low)
        shift = walk_ref[done] + REACH
        place = iota((LANES, LANES), 0) + iota((LANES, LANES), 1) - shift
        turn = jnp.where((place & (LANES - 1)) == 0, 1.0, 0.0).astype(BF16)
        high = x.astype(BF16)
        mid, low = split(x - high.astype(F32))
        x = mm(high, turn) + (mm(mid, turn) + mm(low, turn))
        lane = iota((SEG_ROWS, LANES), 1)
        label = jnp.full((1, LANES), ids_ref[done], jnp.int32).astype(F32)
        zero = jnp.zeros((1, LANES), F32)
        for part in range(2):
            own = x[part * SEG_ROWS : (part + 1) * SEG_ROWS]
            above = jnp.concatenate([zero, own[: SEG_ROWS - 1]], 0)
            tail = jnp.where(lane[:1] < REACH, own[SEG_ROWS - 1 :], 0.0)
            own = jnp.where(lane < shift, above, own)
            slot = 2 * done + part
            for dev in range(devices):
                first = dev * span // LANES
                for r in range(rows_sent):
                    at = first + r
                    row = own[at : at + 1] if at < SEG_ROWS else tail if at == SEG_ROWS else zero
                    if r == rows_sent - 1:
                        row = jnp.where(lane[:1] == LANES - 1, label, row)
                    send[dev, r, pl.ds(slot, 1), :] = row

    finish(jnp.maximum(block - 1, 0))

    swap = swap_ref[...]
    for ch in range(chunks):
        at = ch * CHUNK
        turned = mm(s_ref[0, at : at + CHUNK, :], swap, ((0,), (0,)))
        lhs_ref[:, at : at + CHUNK] = turned.astype(BF16)
        late = at + SEG_ROWS
        rhs_ref[ch, CHUNK:, :] = mm(swap, e_ref[0, late : late + CHUNK, :]).astype(BF16)
        rhs_ref[ch, :CHUNK, :] = mm(swap, e_ref[0, at : at + CHUNK, :]).astype(BF16)

    def product(a):
        off = (SEG_ROWS - a) * SEG_ROWS
        rhs = jnp.concatenate([rhs_ref[ch, off : off + CHUNK, :] for ch in range(chunks)], 0)
        g = mm(lhs_ref[...], rhs)
        return (
            g[:LANES, :LANES] + g[LANES:, LANES:],
            g[LANES:, :LANES] - g[:LANES, LANES:],
        )

    lower = iota((LANES, LANES), 1) <= iota((LANES, LANES), 0)
    later = product(SEG_ROWS)
    for a in reversed(range(SEG_ROWS)):
        here = product(a)
        for part in range(2):
            x = jnp.where(lower, here[part], later[part])
            half = LANES // 2
            while half >= 8:
                x = x[:half] + pltpu.roll(x[half:], LANES - half, 1)
                half //= 2
            diag_ref[part, a] = x
        later = here

    @pl.when(block == blocks - 1)
    def _():
        finish(block)
        pl.semaphore_wait(barrier, devices - 1)
        copies = []
        for k, peer in enumerate(peers):
            copy = pltpu.make_async_remote_copy(
                src_ref=send.at[peer],
                dst_ref=got.at[me],
                send_sem=send_sem.at[k],
                recv_sem=recv_sem.at[k],
                device_id={"tm": peer},
                device_id_type=MESH,
            )
            copy.start()
            copies.append(copy)
        got[me] = send[me]
        for copy in copies:
            copy.wait()
        out_ref[...] = got[...]


def cosine(count):
    wrapped = ((count + DOP // 2) & (DOP - 1)) - DOP // 2
    z = (DOP // 4 - jnp.abs(wrapped)).astype(F32) * (2.0 * math.pi / DOP)
    z2 = z * z
    poly = -1.0 / 39916800.0
    for c in (1.0 / 362880.0, -1.0 / 5040.0, 1.0 / 120.0, -1.0 / 6.0, 1.0):
        poly = poly * z2 + c
    return z * poly


def map_kernel(
    span, got, guard_ref, size_ref, dft_high, dft_low, tab_high, tab_low, ker_high, ker_low,
    out_ref, power_ref, coef_ref,
):
    me = lax.axis_index("tm")
    devices, rows_sent, per = got.shape[:3]
    total = devices * per // 2
    if span % LANES == 0:
        lead, width = REACH, span + 2 * REACH
    else:
        width = rows_sent * LANES
        lead = pl.multiple_of(lax.rem(me * span, LANES) + REACH, 8)
    guard = guard_ref[...].astype(F32)
    size = size_ref[...].astype(F32)
    guard = jnp.transpose(jnp.broadcast_to(guard, (LANES, span)))
    outer = guard + jnp.transpose(jnp.broadcast_to(size, (LANES, span)))
    dist = iota((span, LANES), 1).astype(F32)
    inside = jnp.where((dist > guard) & (dist <= outer), 1.0, 0.0).astype(BF16)
    kernel = mm(inside, ker_high[...]) + mm(inside, ker_low[...])
    guard, outer = guard[:, :1], outer[:, :1]
    dist = jnp.abs(iota((span, width), 1) - lead - iota((span, width), 0)).astype(F32)
    band = jnp.where((dist > guard) & (dist <= outer), 1.0, 0.0).astype(BF16)
    spot = (me * span + iota((span, 1), 0)).astype(F32)
    last = (D - 1) - spot
    count = jnp.minimum(spot, outer) - jnp.minimum(spot, guard)
    count = count + jnp.minimum(last, outer) - jnp.minimum(last, guard)
    weight = 1.0 / (count + 2.0 * (outer - guard))

    rows = [[got[dev, r] for r in range(rows_sent)] for dev in range(devices)]
    stacked = jnp.concatenate([jnp.concatenate(r, 1) for r in rows], 0)
    ids = stacked[:, rows_sent * LANES - 1 :].astype(jnp.int32)
    shape = (devices * per, DOP)
    turns = ids * iota(shape, 1) - (DOP // 4) * (iota(shape, 0) & 1)
    mix_re_high, mix_re_low = split(cosine(turns))
    mix_im_high, mix_im_low = split(cosine(turns + DOP // 4))
    corr = jnp.transpose(stacked)[:width]
    corr_high, corr_low = split(corr)
    norm = 1.0 / (total * SEGS * D)
    re = mm(corr_high, mix_re_high) + (mm(corr_low, mix_re_high) + mm(corr_high, mix_re_low))
    im = mm(corr_high, mix_im_high) + (mm(corr_low, mix_im_high) + mm(corr_high, mix_im_low))
    power = (re * re + im * im) * norm
    floor = jnp.sum(corr * corr, axis=1, keepdims=True) * norm
    coef = mm3(power, dft_high[...], dft_low[...])
    if span % LANES == 0:
        power_c = power[lead : lead + span]
        coef_c = coef[lead : lead + span]
        floor_c = floor[lead : lead + span]
    else:
        power_ref[:, :DOP] = power
        power_ref[:, DOP:] = jnp.broadcast_to(floor, (width, LANES))
        coef_ref[...] = coef
        power_c = power_ref[pl.ds(lead, span), :DOP]
        floor_c = power_ref[pl.ds(lead, span), DOP:][:, :1]
        coef_c = coef_ref[pl.ds(lead, span), :]
    coef_high, coef_low = split(coef)
    sums = mm(band, coef_high) + mm(band, coef_low) + coef_c * kernel
    noise = mm3(sums, tab_high[...], tab_low[...]) * weight
    out_ref[...] = (power_c - floor_c) / (0.25 + noise)


def np_split(x):
    high = x.astype(BF16)
    return jnp.asarray(high), jnp.asarray((x - high.astype(np.float64)).astype(BF16))


def tables(total):
    lag, freq = np.arange(total), np.arange(DOP)
    angle = 2.0 * np.pi / DOP * ((lag[:, None] * freq[None, :]) % DOP)
    tab = np.concatenate([np.cos(angle), np.sin(angle)], 0)
    scale = np.where(lag == 0, 1.0, 2.0) / DOP
    dft = tab.T * np.concatenate([scale, scale])[None, :]
    dist = np.arange(LANES)
    ker = 2.0 * np.cos(2.0 * np.pi / DOP * ((dist[:, None] * lag[None, :]) % DOP))
    ker = np.concatenate([ker, ker], 1)
    return (*np_split(dft), *np_split(tab), *np_split(ker))


def body(surveillance, ref_samples, block_ids, walk, cfar_guard, cfar_window):
    blocks, rows_all = surveillance.shape[:2]
    devices = lax.axis_size("tm")
    total = blocks * devices
    span = D // devices
    rows_sent = window_rows(span)
    chunks = rows_all // CHUNK
    send_shape = (devices, rows_sent, 2 * blocks, LANES)
    smem = pl.BlockSpec(memory_space=pltpu.SMEM)
    vmem = pl.BlockSpec(memory_space=pltpu.VMEM)
    place = np.arange(CHUNK)
    swap = place[None, :] == (place % SEG_ROWS * SEG_ROWS + place // SEG_ROWS)[:, None]
    pick = np.arange(2 * SEG_ROWS)[:, None] == (np.arange(16 * SEG_ROWS) // 8)[None, :]
    windows = pl.pallas_call(
        functools.partial(correlate_kernel, span),
        grid=(blocks,),
        out_shape=jax.ShapeDtypeStruct(send_shape, F32),
        in_specs=[
            smem,
            smem,
            pl.BlockSpec((1,) + surveillance.shape[1:], lambda j: (j, 0, 0)),
            pl.BlockSpec((1,) + ref_samples.shape[1:], lambda j: (j, 0, 0)),
            vmem,
            vmem,
        ],
        out_specs=vmem,
        scratch_shapes=[
            pltpu.VMEM((2 * LANES, rows_all), BF16),
            pltpu.VMEM((chunks, 2 * CHUNK, 2 * LANES), BF16),
            pltpu.VMEM((2, SEG_ROWS, 8, LANES), F32),
            pltpu.VMEM(send_shape, F32),
            pltpu.VMEM(send_shape, F32),
            pltpu.SemaphoreType.DMA((devices,)),
            pltpu.SemaphoreType.DMA((devices,)),
        ],
        compiler_params=pltpu.CompilerParams(
            dimension_semantics=("arbitrary",), collective_id=0, has_side_effects=True
        ),
        name="correlate",
    )(walk, block_ids, surveillance, ref_samples, jnp.asarray(swap.astype(BF16)), jnp.asarray(pick.astype(BF16)))
    width = span + 2 * REACH if span % LANES == 0 else rows_sent * LANES
    return pl.pallas_call(
        functools.partial(map_kernel, span),
        out_shape=jax.ShapeDtypeStruct((span, DOP), F32),
        in_specs=[vmem] * 9,
        out_specs=vmem,
        scratch_shapes=[
            pltpu.VMEM((width, DOP + LANES), F32),
            pltpu.VMEM((width, 2 * total), F32),
        ],
        name="map",
    )(windows, cfar_guard.reshape(1, span), cfar_window.reshape(1, span), *tables(total))


def solution(mesh):
    in_specs = (
        P(("chan", "tm"), None, None),
        P("tm", None, None),
        P("tm"),
        P("tm"),
        P("tm"),
        P("tm"),
    )
    out_specs = P(("chan", "tm"), None)
    return jax.shard_map(body, mesh=mesh, in_specs=in_specs, out_specs=out_specs, check_vma=False)
```
